32 devices in a mesh: groups: 2 (over y), lon: 4 (over z), lat: 2 (over x), dp: 2 (over core).
Axes of the slice: x: 2, y: 2, z: 4, core: 2. Of those that a mesh axis runs over, the one named last changes fastest.
Arguments:
- inputs: bfloat16 [4, 128, 1024, 128], P(('groups', 'dp'), 'lat', 'lon'), parts along dimension 0, may hold values from -6 to 6
- cotangent: bfloat16 [4, 128, 1024, 128], P(('groups', 'dp'), 'lat', 'lon'), parts along dimension 0, may hold values from -6 to 6
- kernel_dw: bfloat16 [7, 7, 128], replicated, may hold values from -0.875 to 0.875
- bias_dw: float32 [128], replicated, may hold values from -3 to 3
- gain: float32 [128], replicated, may hold values from 0.1 to 1.9
- shift_ln: float32 [128], replicated, may hold values from -2 to 2
- w_in: bfloat16 [128, 256], replicated, may hold values from -0.5 to 0.5
- b_in: float32 [256], replicated, may hold values from -2 to 2
- w_out: bfloat16 [256, 128], replicated, may hold values from -0.375 to 0.375
- ocean_mask: int32 [2, 16], P('lat', 'lon'), may hold values from 0 to 1, as said below
Outputs:
- grad_inputs: bfloat16 [4, 128, 1024, 128], P(('groups', 'dp'), 'lat', 'lon'), parts along dimension 0
- grad_w_in: float32 [256, 256], P(('groups', 'dp')), parts along dimension 0
- grad_w_out: float32 [512, 128], P(('groups', 'dp')), parts along dimension 0
- grad_kernel: float32 [14, 7, 128], P('groups'), parts along dimension 0
- grad_bias_dw: float32 [256], P('groups'), parts along dimension 0
- grad_gain: float32 [256], P('groups'), parts along dimension 0
- grad_shift: float32 [256], P('groups'), parts along dimension 0
- grad_b_in: float32 [512], P('groups'), parts along dimension 0
The draws below stay inside these ranges and needn't reach their ends.
There are 2 independent parts, one for each index of `groups`. The reference program is written for one: setup_inputs(seed, part) draws one part's arguments, and reference() takes and returns one part's arrays. A program takes and returns all parts, laid end to end along the dimension named above; an argument that names none is the same for every part. Nothing has to cross between parts.
Inputs may be any that keep to these rules, and one draw needn't show every extreme that they name: `ocean_mask`: every block of the northernmost block row (index 1) is ocean, and each aligned run of 4 blocks of a block row holds at least one ocean block.
All inputs are finite; a program needn't handle non-finite values.
Results may differ from the reference program's by a relative error of at most 0.0056.
Values may be sent and summed in bfloat16 or wider, within the bound.
A program may use at most 128 MiB of HBM per device.

```python
import math
import jax
import jax.numpy as jnp
from jax import lax

BLK = 64
BLOCKS_DEV = 4
C = 128
HID = 256
KS = 7
BATCH = 2
H = 128
W = 1024
HB = 2
WB = 16


def draw_ocean_mask(key, part):
    key_shift, key_roll, key_pick = jax.random.split(jax.random.fold_in(key, 17), 3)
    columns = jnp.arange(WB, dtype=jnp.int32)
    offset = jax.random.randint(key_shift, (), 0, WB, dtype=jnp.int32)
    wave = (columns + offset) % WB
    triangle = jnp.minimum(wave, WB - wave)
    limit = 10 + 160 * triangle // WB
    rolled = jax.random.randint(key_roll, (HB, WB), 0, 100, dtype=jnp.int32)
    ocean = rolled < limit[None, :]
    picked = jax.random.randint(key_pick, (HB, WB // BLOCKS_DEV), 0, BLOCKS_DEV, dtype=jnp.int32)
    forced = (columns % BLOCKS_DEV)[None, :] == jnp.repeat(picked, BLOCKS_DEV, axis=1)
    northern = (jnp.arange(HB, dtype=jnp.int32) == HB - 1)[:, None]
    return jnp.where(forced | northern | ocean, 1, 0).astype(jnp.int32)


def steps_of(stream_key, shape, cuts, smallest, top_value):
    loudness, own = 1.0, jax.random.fold_in(stream_key, 6)
    for axis_at, blocks in cuts:
        draws = jnp.exp(jax.random.uniform(jax.random.fold_in(own, axis_at), (blocks,), jnp.float32, smallest / len(cuts), top_value / len(cuts)))
        loudness = loudness * jnp.repeat(draws, shape[axis_at] // blocks).reshape([-1 if axis == axis_at else 1 for axis in range(len(shape))])
    return loudness


def normal_values(rng, shape, deviation, reach, shards=(), held_as=jnp.bfloat16):
    drawn = deviation * jax.random.normal(rng, shape, jnp.float32)
    if shards:
        drawn = drawn * steps_of(rng, shape, shards, -0.22, 0.18)
    return jnp.clip(drawn, -reach, reach).astype(held_as)


def setup_inputs(seed: int = 0, part: int = 0) -> dict:
    seeds = jax.random.split(jax.random.key(seed), 11)
    own_keys = jax.random.split(jax.random.fold_in(seeds[10], part), 11)
    return {
        "inputs": normal_values(own_keys[0], (BATCH, H, W, C), 1.0, 6.0, ((0, 2), (1, 2), (2, 4))),
        "cotangent": normal_values(own_keys[1], (BATCH, H, W, C), 1.0, 6.0, ((0, 2), (1, 2), (2, 4))),
        "kernel_dw": normal_values(seeds[2], (KS, KS, C), (KS * KS) ** -0.5, 0.875),
        "bias_dw": normal_values(seeds[3], (C,), 0.5, 3.0, (), jnp.float32),
        "gain": jnp.clip(1.0 + 0.18 * jax.random.normal(seeds[4], (C,), jnp.float32), 0.1, 1.9),
        "shift_ln": normal_values(seeds[5], (C,), 0.3, 2.0, (), jnp.float32),
        "w_in": normal_values(seeds[6], (C, HID), C ** -0.5, 0.5),
        "b_in": normal_values(seeds[7], (HID,), 0.3, 2.0, (), jnp.float32),
        "w_out": normal_values(seeds[8], (HID, C), HID ** -0.5, 0.375),
        "ocean_mask": draw_ocean_mask(jax.random.fold_in(seeds[10], 71), part),
    }


EPS = 1e-06
GELU_K = 0.7978845608
GELU_C = 0.044715

def extend(field):
    half = KS // 2
    height = field.shape[0]
    south = jnp.zeros((half,) + field.shape[1:], field.dtype)
    north = field[height - half:][::-1, ::-1, :]
    framed = jnp.concatenate([south, field, north], 0)
    width = field.shape[1]
    return jnp.concatenate([framed[:, width - half:], framed, framed[:, :half]], 1)

def conv_valid(extended, kernel):
    return lax.conv_general_dilated(extended, kernel[:, :, None, :], (1, 1), 'VALID', dimension_numbers=('NHWC', 'HWIO', 'NHWC'), feature_group_count=extended.shape[3], preferred_element_type=jnp.float32)

def kernel_grad(extended, delta):
    out = lax.conv_general_dilated(extended[None], delta[:, :, None, :], (1, 1), 'VALID', dimension_numbers=('NHWC', 'HWIO', 'NHWC'), feature_group_count=extended.shape[2], preferred_element_type=jnp.float32)
    return out[0]

def cell_grads(ycells, gcells, maskval, gain, shift_ln, w_in, b_in, w_out):
    center = ycells - lax.optimization_barrier(jnp.mean(ycells, -1, keepdims=True))
    rstd = lax.rsqrt(lax.optimization_barrier(jnp.mean(center * center, -1, keepdims=True)) + EPS)
    nhat = center * rstd
    normed = (nhat * gain + shift_ln).astype(jnp.bfloat16)
    pre = jnp.dot(normed, w_in, preferred_element_type=jnp.float32) + b_in
    tangent = jnp.tanh(GELU_K * (pre + GELU_C * pre * pre * pre))
    act = (0.5 * pre * (1.0 + tangent)).astype(jnp.bfloat16)
    outgrad = (gcells.astype(jnp.float32) * maskval).astype(jnp.bfloat16)
    g_out = lax.dot_general(act, outgrad, (((0,), (0,)), ((), ())), preferred_element_type=jnp.float32)
    dact = lax.dot_general(outgrad, w_out, (((1,), (1,)), ((), ())), preferred_element_type=jnp.float32)
    slope = 0.5 * (1.0 + tangent) + 0.5 * pre * (1.0 - tangent * tangent) * GELU_K * (1.0 + 3.0 * GELU_C * pre * pre)
    dpre = dact * slope
    dpre_b = dpre.astype(jnp.bfloat16)
    g_in = lax.dot_general(normed, dpre_b, (((0,), (0,)), ((), ())), preferred_element_type=jnp.float32)
    g_bin = lax.optimization_barrier(jnp.sum(dpre, 0))
    dnorm = lax.dot_general(dpre_b, w_in, (((1,), (1,)), ((), ())), preferred_element_type=jnp.float32)
    g_gain = lax.optimization_barrier(jnp.sum(dnorm * nhat, 0))
    g_shift = lax.optimization_barrier(jnp.sum(dnorm, 0))
    dscaled = dnorm * gain
    delta = rstd * (dscaled - lax.optimization_barrier(jnp.mean(dscaled, -1, keepdims=True)) - nhat * lax.optimization_barrier(jnp.mean(dscaled * nhat, -1, keepdims=True)))
    return (delta.astype(jnp.bfloat16), (g_in, g_bin, g_out, g_gain, g_shift))

def to_blocks(field):
    height, width, chans = field.shape
    parts = field.reshape(height // BLK, BLK, width // BLK, BLK, chans).transpose(0, 2, 1, 3, 4)
    return parts.reshape(-1, BLK * BLK, chans)

def from_blocks(parts, height, width):
    chans = parts.shape[-1]
    grid = parts.reshape(height // BLK, width // BLK, BLK, BLK, chans).transpose(0, 2, 1, 3, 4)
    return grid.reshape(height, width, chans)

def reference(inputs, cotangent, kernel_dw, bias_dw, gain, shift_ln, w_in, b_in, w_out, ocean_mask):
    batch, height, width, chans = inputs.shape
    hidden = w_in.shape[1]
    half = KS // 2
    flat_mask = ocean_mask.reshape(-1).astype(jnp.float32)
    totals = (jnp.zeros((chans, hidden), jnp.float32), jnp.zeros((hidden,), jnp.float32), jnp.zeros((hidden, chans), jnp.float32), jnp.zeros((chans,), jnp.float32), jnp.zeros((chans,), jnp.float32))
    g_kernel = jnp.zeros((KS, KS, chans), jnp.float32)
    g_bias = jnp.zeros((chans,), jnp.float32)

    def step(carry, items):
        ycells, gcells, maskval = items
        delta, grads = cell_grads(ycells, gcells, maskval, gain, shift_ln, w_in, b_in, w_out)
        return (tuple((c + g for c, g in zip(carry, grads))), delta)
    results = []
    for sample in range(batch):
        extended = extend(inputs[sample])
        field_y = conv_valid(extended[None], kernel_dw)[0] + bias_dw
        totals, deltas = lax.scan(step, totals, (to_blocks(field_y), to_blocks(cotangent[sample]), flat_mask))
        delta = from_blocks(deltas, height, width)
        g_kernel = g_kernel + kernel_grad(extended, delta)
        g_bias = g_bias + lax.optimization_barrier(jnp.sum(delta.astype(jnp.float32), (0, 1)))
        spread = extend(delta)
        direct_part = spread.at[height + half:].set(jnp.zeros_like(spread[height + half:]))
        direct = conv_valid(direct_part[None], kernel_dw[::-1, ::-1])[0]
        fold_part = jnp.concatenate([jnp.zeros_like(spread[height - half:height + half]), spread[height + half:]], 0)
        fold = conv_valid(fold_part[None], kernel_dw)[0]
        total = cotangent[sample].astype(jnp.float32) + direct
        total = total.at[height - half:].add(fold)
        results.append(total.astype(jnp.bfloat16))
    scale = 1.0 / math.sqrt(batch * height * width)
    g_in, g_bin, g_out, g_gain, g_shift = totals
    return (jnp.stack(results), g_in * scale, g_out * scale, g_kernel * scale, g_bias * scale, g_gain * scale, g_shift * scale, g_bin * scale)
```

```python
import math

import jax
import jax.numpy as jnp
from jax import lax
from jax.experimental import pallas as pl
from jax.experimental.pallas import tpu as pltpu
from jax.sharding import PartitionSpec as P

KS = 7
HALF = 3
EPS = 1e-06
GELU_K = 0.7978845608
GELU_C = 0.044715
OFF = 8
ROWS_OUT = 8
COLS_OUT = 32
CELL_ROWS = 2
F32 = jnp.float32
BF16 = jnp.bfloat16


def load_extended(ext, tile, south, north, west, east):
    rows, cols, _ = tile.shape

    def fill(r, carry):
        ext[r + HALF, OFF : OFF + cols, :] = tile[r].astype(F32)
        return carry

    lax.fori_loop(0, rows, fill, 0)
    for m in range(HALF):
        ext[m, OFF : OFF + cols, :] = south[m].astype(F32)
        ext[rows + HALF + m, OFF : OFF + cols, :] = north[m].astype(F32)

    def sides(r, carry):
        ext[r, OFF - HALF : OFF, :] = west[r].astype(F32)
        ext[r, OFF + cols : OFF + cols + HALF, :] = east[r].astype(F32)
        return carry

    lax.fori_loop(0, rows + 2 * HALF, sides, 0)


def conv_steps(ext, taps, rows, cols, flip, finish):
    chunks = cols // COLS_OUT

    def step(i, carry):
        r0 = (i // chunks) * ROWS_OUT
        c0 = pl.multiple_of((i % chunks) * COLS_OUT, COLS_OUT)
        acc = [None] * ROWS_OUT
        for rho in range(ROWS_OUT + KS - 1):
            for b in range(KS):
                v = ext[r0 + rho, pl.ds(c0 + (OFF - HALF + b), COLS_OUT), :]
                v = v.reshape(COLS_OUT // 8, 8, v.shape[-1])
                for a in range(KS):
                    out = rho - a
                    if 0 <= out < ROWS_OUT:
                        t = a * KS + b
                        k = taps[KS * KS - 1 - t if flip else t]
                        term = v * k[None]
                        acc[out] = term if acc[out] is None else acc[out] + term
            if rho >= KS - 1:
                out = rho - (KS - 1)
                finish(r0 + out, c0, acc[out].reshape(COLS_OUT, acc[out].shape[-1]))
        return carry

    lax.fori_loop(0, (rows // ROWS_OUT) * chunks, step, 0)


def partial_sum(x):
    return jnp.sum(x.reshape(x.shape[0] // 8, 8, x.shape[1]), axis=0)


def cells_kernel(
    tile, south, north, west, east, cot, mask, taps, bias, gain, shift, w_in, w_in_t, b_in, w_out_t,
    dy, g_in, g_out, g_chan, g_bin,
    ext, y, s_chan, s_bin,
):
    rows, cols, chans = tile.shape
    hidden = w_in.shape[1]
    load_extended(ext, tile, south, north, west, east)
    bias_row = bias[...]

    def finish(r, c0, acc):
        y[r, pl.ds(c0, COLS_OUT), :] = acc + bias_row

    conv_steps(ext, taps, rows, cols, False, finish)
    g_in[...] = jnp.zeros_like(g_in)
    g_out[...] = jnp.zeros_like(g_out)
    s_chan[...] = jnp.zeros_like(s_chan)
    s_bin[...] = jnp.zeros_like(s_bin)
    count = CELL_ROWS * cols
    inv = 1.0 / chans

    def step(i, carry):
        r0 = i * CELL_ROWS
        yc = y[pl.ds(r0, CELL_ROWS)].reshape(count, chans)
        center = yc - jnp.sum(yc, -1, keepdims=True) * inv
        rstd = lax.rsqrt(jnp.sum(center * center, -1, keepdims=True) * inv + EPS)
        nhat = center * rstd
        normed = (nhat * gain[...] + shift[...]).astype(BF16)
        pre = jnp.dot(normed, w_in[...], preferred_element_type=F32) + b_in[...]
        square = pre * pre
        t = jnp.tanh(pre * (GELU_K + (GELU_K * GELU_C) * square))
        h = 0.5 + 0.5 * t
        act = pre * h
        slope = h + act * (1.0 - h) * (2.0 * GELU_K + (6.0 * GELU_K * GELU_C) * square)
        og = (cot[pl.ds(r0, CELL_ROWS)] * mask[...][None]).reshape(count, chans)
        g_out[...] += lax.dot_general(
            act.astype(BF16), og, (((0,), (0,)), ((), ())), preferred_element_type=F32
        )
        dpre = jnp.dot(og, w_out_t[...], preferred_element_type=F32) * slope
        dpre_b = dpre.astype(BF16)
        s_bin[...] += partial_sum(dpre)
        g_in[...] += lax.dot_general(
            normed, dpre_b, (((0,), (0,)), ((), ())), preferred_element_type=F32
        )
        dnorm = jnp.dot(dpre_b, w_in_t[...], preferred_element_type=F32)
        s_chan[0] += partial_sum(dnorm * nhat)
        s_chan[1] += partial_sum(dnorm)
        dn = dnorm * gain[...]
        m1 = jnp.sum(dn, -1, keepdims=True) * inv
        m2 = jnp.sum(dn * nhat, -1, keepdims=True) * inv
        delta = (rstd * (dn - m1 - nhat * m2)).astype(BF16)
        s_chan[2] += partial_sum(delta.astype(F32))
        dy[pl.ds(r0, CELL_ROWS)] = delta.reshape(CELL_ROWS, cols, chans)
        return carry

    lax.fori_loop(0, rows // CELL_ROWS, step, 0)
    for q in range(3):
        g_chan[q : q + 1, :] = jnp.sum(s_chan[q], axis=0, keepdims=True)
    g_bin[...] = jnp.sum(s_bin[...], axis=0, keepdims=True)


def taps_kernel(tile, south, north, west, east, dy, g_taps, ext, dyf):
    rows, cols, chans = tile.shape
    load_extended(ext, tile, south, north, west, east)
    edge = jnp.zeros((cols, chans), F32)
    for m in range(KS - 1):
        dyf[m] = edge
        dyf[rows + KS - 1 + m] = edge

    def fill(r, carry):
        dyf[r + KS - 1] = dy[r].astype(F32)
        return carry

    lax.fori_loop(0, rows, fill, 0)
    for first, last in ((0, 4), (4, KS)):

        def row_step(rho, acc):
            def col_step(j, acc):
                acc = list(acc)
                for sub in range(4):
                    c0 = pl.multiple_of(j * 32 + sub * 8, 8)
                    d = [dyf[rho + (KS - 1) - a, pl.ds(c0, 8), :] for a in range(first, last)]
                    for b in range(KS):
                        v = ext[rho, pl.ds(c0 + (OFF - HALF + b), 8), :]
                        for q in range(last - first):
                            at = q * KS + b
                            acc[at] = acc[at] + v * d[q]
                return tuple(acc)

            return lax.fori_loop(0, cols // 32, col_step, acc)

        zero = jnp.zeros((8, chans), F32)
        acc = lax.fori_loop(0, rows + KS - 1, row_step, (zero,) * (KS * (last - first)))
        for n, value in enumerate(acc):
            at = first * KS + n
            g_taps[at : at + 1, :] = jnp.sum(value, axis=0, keepdims=True)


def input_kernel(tile, south, north, west, east, cot, taps, is_north, out, ext, fold, total):
    rows, cols, chans = tile.shape
    load_extended(ext, tile, south, north, west, east)
    flag = is_north[0]
    for m in range(HALF):
        row = ext[rows + HALF + m]
        fold[m] = row * flag
        ext[rows + HALF + m] = row * (1.0 - flag)

    def finish(r, c0, acc):
        summed = acc + cot[r, pl.ds(c0, COLS_OUT), :].astype(F32)
        out[r, pl.ds(c0, COLS_OUT), :] = summed.astype(BF16)

        @pl.when(r >= rows - HALF)
        def _():
            total[r - (rows - HALF), pl.ds(c0, COLS_OUT), :] = summed

    conv_steps(ext, taps, rows, cols, True, finish)

    def fold_step(i, carry):
        c0 = pl.multiple_of(i * COLS_OUT, COLS_OUT)
        for m in range(HALF):
            acc = total[m, pl.ds(c0, COLS_OUT), :].reshape(COLS_OUT // 8, 8, chans)
            for n in range(m + 1):
                a = KS - 1 - m + n
                for b in range(KS):
                    v = fold[n, pl.ds(c0 + (OFF - HALF + b), COLS_OUT), :]
                    acc = acc + v.reshape(COLS_OUT // 8, 8, chans) * taps[a * KS + b][None]
            out[rows - HALF + m, pl.ds(c0, COLS_OUT), :] = acc.reshape(COLS_OUT, chans).astype(BF16)
        return carry

    lax.fori_loop(0, cols // COLS_OUT, fold_step, 0)


def halo(tile):
    rows, cols, _ = tile.shape
    lats, lons = lax.axis_size("lat"), lax.axis_size("lon")
    up = [(i, i + 1) for i in range(lats - 1)]
    down = [(i + 1, i) for i in range(lats - 1)]
    south = lax.ppermute(tile[rows - HALF :], "lat", up)
    above = lax.ppermute(tile[:HALF], "lat", down)
    mirror = lax.ppermute(tile[rows - HALF :], "lon", [(i, lons - 1 - i) for i in range(lons)])
    northern = lax.axis_index("lat") == lats - 1
    north = jnp.where(northern, mirror[::-1, ::-1, :], above)
    left = jnp.concatenate([south[:, :HALF], tile[:, :HALF], north[:, :HALF]], 0)
    right = jnp.concatenate([south[:, cols - HALF :], tile[:, cols - HALF :], north[:, cols - HALF :]], 0)
    west = lax.ppermute(right, "lon", [(i, (i + 1) % lons) for i in range(lons)])
    east = lax.ppermute(left, "lon", [((i + 1) % lons, i) for i in range(lons)])
    return south, north, west, east


def call(kernel, out_shape, scratch, flops, *args, scalars=0):
    vmem = pl.BlockSpec(memory_space=pltpu.VMEM)
    smem = pl.BlockSpec(memory_space=pltpu.SMEM)
    return pl.pallas_call(
        kernel,
        out_shape=out_shape,
        in_specs=[vmem] * (len(args) - scalars) + [smem] * scalars,
        out_specs=jax.tree.map(lambda _: vmem, out_shape),
        scratch_shapes=scratch,
        compiler_params=pltpu.CompilerParams(vmem_limit_bytes=56 * 1024 * 1024),
        cost_estimate=pl.CostEstimate(flops=flops, bytes_accessed=12 << 20, transcendentals=0),
    )(*args)


def local(inputs, cotangent, kernel_dw, bias_dw, gain, shift_ln, w_in, b_in, w_out, ocean_mask):
    batch, rows, cols, chans = inputs.shape
    hidden = w_in.shape[1]
    shape = jax.ShapeDtypeStruct
    taps = jnp.broadcast_to(kernel_dw.astype(F32).reshape(KS * KS, 1, chans), (KS * KS, 8, chans))
    blocks = ocean_mask.reshape(-1)
    mask = jnp.broadcast_to(
        jnp.repeat(blocks, cols // blocks.shape[0])[:, None], (cols, chans)
    ).astype(BF16)
    ext_shape = pltpu.VMEM((rows + 2 * HALF, cols + 2 * OFF, chans), F32)
    northern = lax.axis_index("lat") == lax.axis_size("lat") - 1
    is_north = jnp.where(northern, 1.0, 0.0).astype(F32).reshape(1)
    work = 2 * KS * KS * rows * cols * chans * 128
    sums, grads = None, []
    for n in range(batch):
        tile, cot = inputs[n], cotangent[n]
        frame = halo(tile)
        dy, g_in, g_out, g_chan, g_bin = call(
            cells_kernel,
            (
                shape(tile.shape, BF16),
                shape((chans, hidden), F32),
                shape((hidden, chans), F32),
                shape((3, chans), F32),
                shape((1, hidden), F32),
            ),
            [
                ext_shape,
                pltpu.VMEM((rows, cols, chans), F32),
                pltpu.VMEM((3, 8, chans), F32),
                pltpu.VMEM((8, hidden), F32),
            ],
            work,
            tile, *frame, cot, mask, taps, bias_dw[None], gain[None], shift_ln[None],
            w_in, w_in.T, b_in[None], w_out.T,
        )
        g_taps = call(
            taps_kernel,
            shape((KS * KS, chans), F32),
            [ext_shape, pltpu.VMEM((rows + 2 * (KS - 1), cols, chans), F32)],
            work,
            tile, *frame, dy,
        )
        grads.append(
            call(
                input_kernel,
                shape(tile.shape, BF16),
                [
                    ext_shape,
                    pltpu.VMEM((HALF, cols + 2 * OFF, chans), F32),
                    pltpu.VMEM((HALF, cols, chans), F32),
                ],
                work,
                dy, *halo(dy), cot, taps, is_north, scalars=1,
            )
        )
        own = (g_in, g_out, g_taps, g_chan, g_bin)
        sums = own if sums is None else tuple(s + o for s, o in zip(sums, own))
    g_in, g_out, g_taps, g_chan, g_bin = sums
    axes = ("lon", "lat", "dp")
    s_in, s_out, s_chan, s_bin = lax.psum((g_in, g_out, g_chan, g_bin), axes)
    s_taps = lax.psum(g_taps, axes)
    cells_all = lax.axis_size("dp") * batch * lax.axis_size("lat") * rows * lax.axis_size("lon") * cols
    scale = 1.0 / math.sqrt(cells_all)
    in_share = chans // lax.axis_size("dp")
    out_share = hidden // lax.axis_size("dp")
    position = lax.axis_index("dp")
    s_in = lax.dynamic_slice_in_dim(s_in, position * in_share, in_share, 0)
    s_out = lax.dynamic_slice_in_dim(s_out, position * out_share, out_share, 0)
    return (
        jnp.stack(grads),
        s_in * scale,
        s_out * scale,
        s_taps.reshape(KS, KS, chans) * scale,
        s_chan[2] * scale,
        s_chan[0] * scale,
        s_chan[1] * scale,
        s_bin[0] * scale,
    )


def solution(mesh):
    field = P(("groups", "dp"), "lat", "lon", None)
    placed = (field, field, P(), P(), P(), P(), P(), P(), P(), P("lat", "lon"))
    return jax.shard_map(
        local,
        mesh=mesh,
        in_specs=placed,
        out_specs=(
            field,
            P(("groups", "dp"), None),
            P(("groups", "dp"), None),
            P("groups", None, None),
            P("groups"),
            P("groups"),
            P("groups"),
            P("groups"),
        ),
        check_vma=False,
    )
```

```python
import math

import jax
import jax.numpy as jnp
from jax import lax
from jax.experimental import pallas as pl
from jax.experimental.pallas import tpu as pltpu
from jax.sharding import PartitionSpec as P

KS = 7
HALF = 3
EPS = 1e-06
GELU_K = 0.7978845608
GELU_C = 0.044715
OFF = 8
ROWS_OUT = 8
COLS_OUT = 32
CELL_ROWS = 2
F32 = jnp.float32
BF16 = jnp.bfloat16


def load_extended(ext, tile, south, north, west, east):
    rows, cols, _ = tile.shape

    def fill(r, carry):
        ext[r + HALF, OFF : OFF + cols, :] = tile[r].astype(F32)
        return carry

    lax.fori_loop(0, rows, fill, 0)
    for m in range(HALF):
        ext[m, OFF : OFF + cols, :] = south[m].astype(F32)
        ext[rows + HALF + m, OFF : OFF + cols, :] = north[m].astype(F32)

    def sides(r, carry):
        ext[r, OFF - HALF : OFF, :] = west[r].astype(F32)
        ext[r, OFF + cols : OFF + cols + HALF, :] = east[r].astype(F32)
        return carry

    lax.fori_loop(0, rows + 2 * HALF, sides, 0)


def conv_steps(ext, taps, rows, cols, flip, finish):
    chunks = cols // COLS_OUT

    def step(i, carry):
        r0 = (i // chunks) * ROWS_OUT
        c0 = pl.multiple_of((i % chunks) * COLS_OUT, COLS_OUT)
        acc = [None] * ROWS_OUT
        for rho in range(ROWS_OUT + KS - 1):
            for b in range(KS):
                v = ext[r0 + rho, pl.ds(c0 + (OFF - HALF + b), COLS_OUT), :]
                v = v.reshape(COLS_OUT // 8, 8, v.shape[-1])
                for a in range(KS):
                    out = rho - a
                    if 0 <= out < ROWS_OUT:
                        t = a * KS + b
                        k = taps[KS * KS - 1 - t if flip else t]
                        term = v * k[None]
                        acc[out] = term if acc[out] is None else acc[out] + term
            if rho >= KS - 1:
                out = rho - (KS - 1)
                finish(r0 + out, c0, acc[out].reshape(COLS_OUT, acc[out].shape[-1]))
        return carry

    lax.fori_loop(0, (rows // ROWS_OUT) * chunks, step, 0)


def partial_sum(x):
    return jnp.sum(x.reshape(x.shape[0] // 8, 8, x.shape[1]), axis=0)


def cells_kernel(
    tile, south, north, west, east, cot, mask, taps, bias, gain, shift, w_in, w_in_t, b_in, w_out_t,
    dy, g_in, g_out, g_chan, g_bin,
    ext, y, s_chan, s_bin,
):
    rows, cols, chans = tile.shape
    hidden = w_in.shape[1]
    load_extended(ext, tile, south, north, west, east)
    bias_row = bias[...]

    def finish(r, c0, acc):
        y[r, pl.ds(c0, COLS_OUT), :] = acc + bias_row

    conv_steps(ext, taps, rows, cols, False, finish)
    g_in[...] = jnp.zeros_like(g_in)
    g_out[...] = jnp.zeros_like(g_out)
    s_chan[...] = jnp.zeros_like(s_chan)
    s_bin[...] = jnp.zeros_like(s_bin)
    count = CELL_ROWS * cols
    inv = 1.0 / chans

    def step(i, carry):
        r0 = i * CELL_ROWS
        yc = y[pl.ds(r0, CELL_ROWS)].reshape(count, chans)
        center = yc - jnp.sum(yc, -1, keepdims=True) * inv
        rstd = lax.rsqrt(jnp.sum(center * center, -1, keepdims=True) * inv + EPS)
        nhat = center * rstd
        normed = (nhat * gain[...] + shift[...]).astype(BF16)
        pre = jnp.dot(normed, w_in[...], preferred_element_type=F32) + b_in[...]
        square = pre * pre
        t = jnp.tanh(pre * (GELU_K + (GELU_K * GELU_C) * square))
        h = 0.5 + 0.5 * t
        act = pre * h
        slope = h + act * (1.0 - h) * (2.0 * GELU_K + (6.0 * GELU_K * GELU_C) * square)
        og = (cot[pl.ds(r0, CELL_ROWS)] * mask[...][None]).reshape(count, chans)
        g_out[...] += lax.dot_general(
            act.astype(BF16), og, (((0,), (0,)), ((), ())), preferred_element_type=F32
        )
        dpre = jnp.dot(og, w_out_t[...], preferred_element_type=F32) * slope
        dpre_b = dpre.astype(BF16)
        s_bin[...] += partial_sum(dpre)
        g_in[...] += lax.dot_general(
            normed, dpre_b, (((0,), (0,)), ((), ())), preferred_element_type=F32
        )
        dnorm = jnp.dot(dpre_b, w_in_t[...], preferred_element_type=F32)
        s_chan[0] += partial_sum(dnorm * nhat)
        s_chan[1] += partial_sum(dnorm)
        dn = dnorm * gain[...]
        m1 = jnp.sum(dn, -1, keepdims=True) * inv
        m2 = jnp.sum(dn * nhat, -1, keepdims=True) * inv
        delta = (rstd * (dn - m1 - nhat * m2)).astype(BF16)
        s_chan[2] += partial_sum(delta.astype(F32))
        dy[pl.ds(r0, CELL_ROWS)] = delta.reshape(CELL_ROWS, cols, chans)
        return carry

    lax.fori_loop(0, rows // CELL_ROWS, step, 0)
    for q in range(3):
        g_chan[q : q + 1, :] = jnp.sum(s_chan[q], axis=0, keepdims=True)
    g_bin[...] = jnp.sum(s_bin[...], axis=0, keepdims=True)


def taps_kernel(tile, south, north, west, east, dy, g_taps, ext, dyf):
    rows, cols, chans = tile.shape
    load_extended(ext, tile, south, north, west, east)
    edge = jnp.zeros((cols, chans), F32)
    for m in range(KS - 1):
        dyf[m] = edge
        dyf[rows + KS - 1 + m] = edge

    def fill(r, carry):
        dyf[r + KS - 1] = dy[r].astype(F32)
        return carry

    lax.fori_loop(0, rows, fill, 0)
    for first, last in ((0, 4), (4, KS)):

        def row_step(rho, acc):
            def col_step(j, acc):
                acc = list(acc)
                for sub in range(8):
                    c0 = pl.multiple_of(j * 64 + sub * 8, 8)
                    d = [dyf[rho + (KS - 1) - a, pl.ds(c0, 8), :] for a in range(first, last)]
                    for b in range(KS):
                        v = ext[rho, pl.ds(c0 + (OFF - HALF + b), 8), :]
                        for q in range(last - first):
                            at = q * KS + b
                            acc[at] = acc[at] + v * d[q]
                return tuple(acc)

            return lax.fori_loop(0, cols // 64, col_step, acc)

        zero = jnp.zeros((8, chans), F32)
        acc = lax.fori_loop(0, rows + KS - 1, row_step, (zero,) * (KS * (last - first)))
        for n, value in enumerate(acc):
            at = first * KS + n
            g_taps[at : at + 1, :] = jnp.sum(value, axis=0, keepdims=True)


def input_kernel(tile, south, north, west, east, cot, taps, is_north, out, ext, fold, total):
    rows, cols, chans = tile.shape
    load_extended(ext, tile, south, north, west, east)
    flag = is_north[0]
    for m in range(HALF):
        row = ext[rows + HALF + m]
        fold[m] = row * flag
        ext[rows + HALF + m] = row * (1.0 - flag)

    def finish(r, c0, acc):
        summed = acc + cot[r, pl.ds(c0, COLS_OUT), :].astype(F32)
        out[r, pl.ds(c0, COLS_OUT), :] = summed.astype(BF16)

        @pl.when(r >= rows - HALF)
        def _():
            total[r - (rows - HALF), pl.ds(c0, COLS_OUT), :] = summed

    conv_steps(ext, taps, rows, cols, True, finish)

    def fold_step(i, carry):
        c0 = pl.multiple_of(i * COLS_OUT, COLS_OUT)
        for m in range(HALF):
            acc = total[m, pl.ds(c0, COLS_OUT), :].reshape(COLS_OUT // 8, 8, chans)
            for n in range(m + 1):
                a = KS - 1 - m + n
                for b in range(KS):
                    v = fold[n, pl.ds(c0 + (OFF - HALF + b), COLS_OUT), :]
                    acc = acc + v.reshape(COLS_OUT // 8, 8, chans) * taps[a * KS + b][None]
            out[rows - HALF + m, pl.ds(c0, COLS_OUT), :] = acc.reshape(COLS_OUT, chans).astype(BF16)
        return carry

    lax.fori_loop(0, cols // COLS_OUT, fold_step, 0)


def halo(tile):
    rows, cols, _ = tile.shape
    lats, lons = lax.axis_size("lat"), lax.axis_size("lon")
    up = [(i, i + 1) for i in range(lats - 1)]
    down = [(i + 1, i) for i in range(lats - 1)]
    south = lax.ppermute(tile[rows - HALF :], "lat", up)
    above = lax.ppermute(tile[:HALF], "lat", down)
    mirror = lax.ppermute(tile[rows - HALF :], "lon", [(i, lons - 1 - i) for i in range(lons)])
    northern = lax.axis_index("lat") == lats - 1
    north = jnp.where(northern, mirror[::-1, ::-1, :], above)
    left = jnp.concatenate([south[:, :HALF], tile[:, :HALF], north[:, :HALF]], 0)
    right = jnp.concatenate([south[:, cols - HALF :], tile[:, cols - HALF :], north[:, cols - HALF :]], 0)
    west = lax.ppermute(right, "lon", [(i, (i + 1) % lons) for i in range(lons)])
    east = lax.ppermute(left, "lon", [((i + 1) % lons, i) for i in range(lons)])
    return south, north, west, east


def call(kernel, out_shape, scratch, flops, *args, scalars=0):
    vmem = pl.BlockSpec(memory_space=pltpu.VMEM)
    smem = pl.BlockSpec(memory_space=pltpu.SMEM)
    return pl.pallas_call(
        kernel,
        out_shape=out_shape,
        in_specs=[vmem] * (len(args) - scalars) + [smem] * scalars,
        out_specs=jax.tree.map(lambda _: vmem, out_shape),
        scratch_shapes=scratch,
        compiler_params=pltpu.CompilerParams(vmem_limit_bytes=56 * 1024 * 1024),
        cost_estimate=pl.CostEstimate(flops=flops, bytes_accessed=12 << 20, transcendentals=0),
    )(*args)


def axis_sum(x, axis):
    count = lax.axis_size(axis)
    if count & (count - 1):
        return lax.psum(x, axis)
    step = 1
    while step < count:
        x = x + lax.ppermute(x, axis, [(i, i ^ step) for i in range(count)])
        step *= 2
    return x


def dp_share(x, share):
    count, at = lax.axis_size("dp"), lax.axis_index("dp")
    if count != 2:
        return lax.dynamic_slice_in_dim(lax.psum(x, "dp"), at * share, share, 0)
    mine = lax.dynamic_slice_in_dim(x, at * share, share, 0)
    theirs = lax.dynamic_slice_in_dim(x, (1 - at) * share, share, 0)
    return mine + lax.ppermute(theirs, "dp", [(0, 1), (1, 0)])


def local(inputs, cotangent, kernel_dw, bias_dw, gain, shift_ln, w_in, b_in, w_out, ocean_mask):
    batch, rows, cols, chans = inputs.shape
    hidden = w_in.shape[1]
    shape = jax.ShapeDtypeStruct
    taps = jnp.broadcast_to(kernel_dw.astype(F32).reshape(KS * KS, 1, chans), (KS * KS, 8, chans))
    blocks = ocean_mask.reshape(-1)
    mask = jnp.broadcast_to(
        jnp.repeat(blocks, cols // blocks.shape[0])[:, None], (cols, chans)
    ).astype(BF16)
    ext_shape = pltpu.VMEM((rows + 2 * HALF, cols + 2 * OFF, chans), F32)
    northern = lax.axis_index("lat") == lax.axis_size("lat") - 1
    is_north = jnp.where(northern, 1.0, 0.0).astype(F32).reshape(1)
    work = 2 * KS * KS * rows * cols * chans * 128
    sums, grads = None, []
    for n in range(batch):
        tile, cot = inputs[n], cotangent[n]
        frame = halo(tile)
        dy, g_in, g_out, g_chan, g_bin = call(
            cells_kernel,
            (
                shape(tile.shape, BF16),
                shape((chans, hidden), F32),
                shape((hidden, chans), F32),
                shape((3, chans), F32),
                shape((1, hidden), F32),
            ),
            [
                ext_shape,
                pltpu.VMEM((rows, cols, chans), F32),
                pltpu.VMEM((3, 8, chans), F32),
                pltpu.VMEM((8, hidden), F32),
            ],
            work,
            tile, *frame, cot, mask, taps, bias_dw[None], gain[None], shift_ln[None],
            w_in, w_in.T, b_in[None], w_out.T,
        )
        g_taps = call(
            taps_kernel,
            shape((KS * KS, chans), F32),
            [ext_shape, pltpu.VMEM((rows + 2 * (KS - 1), cols, chans), F32)],
            work,
            tile, *frame, dy,
        )
        grads.append(
            call(
                input_kernel,
                shape(tile.shape, BF16),
                [
                    ext_shape,
                    pltpu.VMEM((HALF, cols + 2 * OFF, chans), F32),
                    pltpu.VMEM((HALF, cols, chans), F32),
                ],
                work,
                dy, *halo(dy), cot, taps, is_north, scalars=1,
            )
        )
        own = (g_in, g_out, g_taps, g_chan, g_bin)
        sums = own if sums is None else tuple(s + o for s, o in zip(sums, own))
    g_in, g_out, g_taps, g_chan, g_bin = sums
    cells_all = lax.axis_size("dp") * batch * lax.axis_size("lat") * rows * lax.axis_size("lon") * cols
    scale = 1.0 / math.sqrt(cells_all)
    in_share = chans // lax.axis_size("dp")
    out_share = hidden // lax.axis_size("dp")
    halves = (
        dp_share(g_in, in_share).reshape(-1, chans),
        dp_share(g_out, out_share),
        axis_sum(jnp.concatenate([g_chan, g_bin.reshape(-1, chans)], 0), "dp"),
    )
    total = jnp.concatenate([*halves, g_taps], 0)
    for axis in ("lat", "lon"):
        total = axis_sum(total, axis)
    in_rows = in_share * hidden // chans
    parts = jnp.split(total, (in_rows, in_rows + out_share, in_rows + out_share + 3, total.shape[0] - KS * KS))
    s_in, s_out, s_chan, s_bin, s_taps = parts
    s_in, s_bin = s_in.reshape(in_share, hidden), s_bin.reshape(1, hidden)
    s_taps = axis_sum(s_taps, "dp")
    return (
        jnp.stack(grads),
        s_in * scale,
        s_out * scale,
        s_taps.reshape(KS, KS, chans) * scale,
        s_chan[2] * scale,
        s_chan[0] * scale,
        s_chan[1] * scale,
        s_bin[0] * scale,
    )


def solution(mesh):
    field = P(("groups", "dp"), "lat", "lon", None)
    placed = (field, field, P(), P(), P(), P(), P(), P(), P(), P("lat", "lon"))
    return jax.shard_map(
        local,
        mesh=mesh,
        in_specs=placed,
        out_specs=(
            field,
            P(("groups", "dp"), None),
            P(("groups", "dp"), None),
            P("groups", None, None),
            P("groups"),
            P("groups"),
            P("groups"),
            P("groups"),
        ),
        check_vma=False,
    )
```

```python
import functools
import math

import jax
import jax.numpy as jnp
from jax import lax
from jax.experimental import pallas as pl
from jax.experimental.pallas import tpu as pltpu
from jax.sharding import PartitionSpec as P

KS = 7
HALF = 3
EPS = 1e-06
GELU_K = 0.7978845608
GELU_C = 0.044715
OFF = 8
ROWS_OUT = 8
COLS_OUT = 32
CELL_ROWS = 4
F32 = jnp.float32
BF16 = jnp.bfloat16


def load_extended(ext, tile, south, north, west, east):
    rows, cols, _ = tile.shape

    def fill(r, carry):
        ext[r + HALF, OFF : OFF + cols, :] = tile[r].astype(F32)
        return carry

    lax.fori_loop(0, rows, fill, 0)
    for m in range(HALF):
        ext[m, OFF : OFF + cols, :] = south[m].astype(F32)
        ext[rows + HALF + m, OFF : OFF + cols, :] = north[m].astype(F32)

    def sides(r, carry):
        ext[r, OFF - HALF : OFF, :] = west[r].astype(F32)
        ext[r, OFF + cols : OFF + cols + HALF, :] = east[r].astype(F32)
        return carry

    lax.fori_loop(0, rows + 2 * HALF, sides, 0)


def conv_steps(ext, taps, rows, cols, flip, finish):
    chunks = cols // COLS_OUT

    def step(i, carry):
        r0 = (i // chunks) * ROWS_OUT
        c0 = pl.multiple_of((i % chunks) * COLS_OUT, COLS_OUT)
        acc = [None] * ROWS_OUT
        for rho in range(ROWS_OUT + KS - 1):
            for b in range(KS):
                v = ext[r0 + rho, pl.ds(c0 + (OFF - HALF + b), COLS_OUT), :]
                v = v.reshape(COLS_OUT // 8, 8, v.shape[-1])
                for a in range(KS):
                    out = rho - a
                    if 0 <= out < ROWS_OUT:
                        t = a * KS + b
                        k = taps[KS * KS - 1 - t if flip else t]
                        term = v * k[None]
                        acc[out] = term if acc[out] is None else acc[out] + term
            if rho >= KS - 1:
                out = rho - (KS - 1)
                finish(r0 + out, c0, acc[out].reshape(COLS_OUT, acc[out].shape[-1]))
        return carry

    lax.fori_loop(0, (rows // ROWS_OUT) * chunks, step, 0)


def partial_sum(x):
    return jnp.sum(x.reshape(x.shape[0] // 8, 8, x.shape[1]), axis=0)


def cells_kernel(
    tile, south, north, west, east, cot, mask, taps, bias, gain, shift, w_in, b_in, w_out,
    dy, g_in, g_out, g_chan, g_bin,
    ext, y, s_chan, s_bin,
):
    rows, cols, chans = tile.shape
    hidden = w_in.shape[1]
    load_extended(ext, tile, south, north, west, east)
    bias_row = bias[...]

    def finish(r, c0, acc):
        y[r, pl.ds(c0, COLS_OUT), :] = acc + bias_row

    conv_steps(ext, taps, rows, cols, False, finish)
    g_in[...] = jnp.zeros_like(g_in)
    g_out[...] = jnp.zeros_like(g_out)
    s_chan[...] = jnp.zeros_like(s_chan)
    s_bin[...] = jnp.zeros_like(s_bin)
    count = CELL_ROWS * cols
    inv = 1.0 / chans

    def step(i, carry):
        r0 = i * CELL_ROWS
        yc = y[pl.ds(r0, CELL_ROWS)].reshape(count, chans)
        center = yc - jnp.sum(yc, -1, keepdims=True) * inv
        rstd = lax.rsqrt(jnp.sum(center * center, -1, keepdims=True) * inv + EPS)
        nhat = center * rstd
        normed = (nhat * gain[...] + shift[...]).astype(BF16)
        pre = jnp.dot(normed, w_in[...], preferred_element_type=F32) + b_in[...]
        square = pre * pre
        t = jnp.tanh(pre * (GELU_K + (GELU_K * GELU_C) * square))
        h = 0.5 + 0.5 * t
        act = pre * h
        slope = h + act * (1.0 - h) * (2.0 * GELU_K + (6.0 * GELU_K * GELU_C) * square)
        og = (cot[pl.ds(r0, CELL_ROWS)] * mask[...][None]).reshape(count, chans)
        g_out[...] += lax.dot_general(
            act.astype(BF16), og, (((0,), (0,)), ((), ())), preferred_element_type=F32
        )
        dact = lax.dot_general(
            og, w_out[...], (((1,), (1,)), ((), ())), preferred_element_type=F32
        )
        dpre = dact * slope
        dpre_b = dpre.astype(BF16)
        s_bin[...] += partial_sum(dpre)
        g_in[...] += lax.dot_general(
            normed, dpre_b, (((0,), (0,)), ((), ())), preferred_element_type=F32
        )
        dnorm = lax.dot_general(
            dpre_b, w_in[...], (((1,), (1,)), ((), ())), preferred_element_type=F32
        )
        s_chan[0] += partial_sum(dnorm * nhat)
        s_chan[1] += partial_sum(dnorm)
        dn = dnorm * gain[...]
        m1 = jnp.sum(dn, -1, keepdims=True) * inv
        m2 = jnp.sum(dn * nhat, -1, keepdims=True) * inv
        delta = (rstd * (dn - m1 - nhat * m2)).astype(BF16)
        s_chan[2] += partial_sum(delta.astype(F32))
        dy[pl.ds(r0, CELL_ROWS)] = delta.reshape(CELL_ROWS, cols, chans)
        return carry

    lax.fori_loop(0, rows // CELL_ROWS, step, 0)
    for q in range(3):
        g_chan[q : q + 1, :] = jnp.sum(s_chan[q], axis=0, keepdims=True)
    g_bin[...] = jnp.sum(s_bin[...], axis=0, keepdims=True)


def taps_kernel(first, last, tile, south, north, west, east, dy, g_taps, ext, dyf):
    rows, cols, chans = tile.shape
    load_extended(ext, tile, south, north, west, east)
    edge = jnp.zeros((cols, chans), F32)
    for m in range(KS - 1):
        dyf[m] = edge
        dyf[rows + KS - 1 + m] = edge

    def fill(r, carry):
        dyf[r + KS - 1] = dy[r].astype(F32)
        return carry

    lax.fori_loop(0, rows, fill, 0)

    def row_step(rho, acc):
        def col_step(j, acc):
            acc = list(acc)
            for sub in range(8):
                c0 = pl.multiple_of(j * 64 + sub * 8, 8)
                d = [dyf[rho + (KS - 1) - a, pl.ds(c0, 8), :] for a in range(first, last)]
                for b in range(KS):
                    v = ext[rho, pl.ds(c0 + (OFF - HALF + b), 8), :]
                    for q in range(last - first):
                        at = q * KS + b
                        acc[at] = acc[at] + v * d[q]
            return tuple(acc)

        return lax.fori_loop(0, cols // 64, col_step, acc)

    zero = jnp.zeros((8, chans), F32)
    acc = lax.fori_loop(0, rows + KS - 1, row_step, (zero,) * (KS * (last - first)))
    for n, value in enumerate(acc):
        g_taps[n : n + 1, :] = jnp.sum(value, axis=0, keepdims=True)


def input_kernel(tile, south, north, west, east, cot, taps, is_north, out, ext, fold, total):
    rows, cols, chans = tile.shape
    load_extended(ext, tile, south, north, west, east)
    flag = is_north[0]
    for m in range(HALF):
        row = ext[rows + HALF + m]
        fold[m] = row * flag
        ext[rows + HALF + m] = row * (1.0 - flag)

    def finish(r, c0, acc):
        summed = acc + cot[r, pl.ds(c0, COLS_OUT), :].astype(F32)
        out[r, pl.ds(c0, COLS_OUT), :] = summed.astype(BF16)

        @pl.when(r >= rows - HALF)
        def _():
            total[r - (rows - HALF), pl.ds(c0, COLS_OUT), :] = summed

    conv_steps(ext, taps, rows, cols, True, finish)

    def fold_step(i, carry):
        c0 = pl.multiple_of(i * COLS_OUT, COLS_OUT)
        for m in range(HALF):
            acc = total[m, pl.ds(c0, COLS_OUT), :].reshape(COLS_OUT // 8, 8, chans)
            for n in range(m + 1):
                a = KS - 1 - m + n
                for b in range(KS):
                    v = fold[n, pl.ds(c0 + (OFF - HALF + b), COLS_OUT), :]
                    acc = acc + v.reshape(COLS_OUT // 8, 8, chans) * taps[a * KS + b][None]
            out[rows - HALF + m, pl.ds(c0, COLS_OUT), :] = acc.reshape(COLS_OUT, chans).astype(BF16)
        return carry

    lax.fori_loop(0, cols // COLS_OUT, fold_step, 0)


def row_halo(tile):
    rows = tile.shape[0]
    lats, lons = lax.axis_size("lat"), lax.axis_size("lon")
    low, high = tile[:HALF], tile[rows - HALF :]
    lat = lax.axis_index("lat")
    if lats % 2:
        south = lax.ppermute(high, "lat", [(i, i + 1) for i in range(lats - 1)])
        above = lax.ppermute(low, "lat", [(i + 1, i) for i in range(lats - 1)])
        mirror = lax.ppermute(high, "lon", [(i, lons - 1 - i) for i in range(lons)])
        north = jnp.where(lat == lats - 1, mirror[::-1, ::-1, :], above)
    else:
        odd = lat % 2 == 1
        first = lax.ppermute(jnp.where(odd, low, high), "lat", [(i, i ^ 1) for i in range(lats)])
        route = []
        for j in range(lons):
            mirrored = lons - 1 - j
            route.append((j * lats + lats - 1, mirrored * lats + lats - 1))
            for i in range(1, lats - 1, 2):
                route.append((j * lats + i, j * lats + i + 1))
                route.append((j * lats + i + 1, j * lats + i))
        second = lax.ppermute(jnp.where(odd, high, low), ("lon", "lat"), route)
        folded = jnp.where(lat == lats - 1, second[::-1, ::-1, :], second)
        south = jnp.where(odd, first, second)
        north = jnp.where(odd, folded, first)
    return south, north


def column_halo(tile, south, north):
    cols, lons = tile.shape[1], lax.axis_size("lon")
    left = jnp.concatenate([south[:, :HALF], tile[:, :HALF], north[:, :HALF]], 0)
    right = jnp.concatenate([south[:, cols - HALF :], tile[:, cols - HALF :], north[:, cols - HALF :]], 0)
    west = lax.ppermute(right, "lon", [(i, (i + 1) % lons) for i in range(lons)])
    east = lax.ppermute(left, "lon", [((i + 1) % lons, i) for i in range(lons)])
    return west, east


def call(kernel, out_shape, scratch, flops, *args, scalars=0):
    vmem = pl.BlockSpec(memory_space=pltpu.VMEM)
    smem = pl.BlockSpec(memory_space=pltpu.SMEM)
    return pl.pallas_call(
        kernel,
        out_shape=out_shape,
        in_specs=[vmem] * (len(args) - scalars) + [smem] * scalars,
        out_specs=jax.tree.map(lambda _: vmem, out_shape),
        scratch_shapes=scratch,
        compiler_params=pltpu.CompilerParams(vmem_limit_bytes=56 * 1024 * 1024),
        cost_estimate=pl.CostEstimate(flops=flops, bytes_accessed=12 << 20, transcendentals=0),
    )(*args)


def axis_sum(x, axis):
    count = lax.axis_size(axis)
    if count & (count - 1):
        return lax.psum(x, axis)
    step = 1
    while step < count:
        x = x + lax.ppermute(x, axis, [(i, i ^ step) for i in range(count)])
        step *= 2
    return x


def dp_share(x, share):
    count, at = lax.axis_size("dp"), lax.axis_index("dp")
    if count != 2:
        return lax.dynamic_slice_in_dim(lax.psum(x, "dp"), at * share, share, 0)
    mine = lax.dynamic_slice_in_dim(x, at * share, share, 0)
    theirs = lax.dynamic_slice_in_dim(x, (1 - at) * share, share, 0)
    return mine + lax.ppermute(theirs, "dp", [(0, 1), (1, 0)])


def local(inputs, cotangent, kernel_dw, bias_dw, gain, shift_ln, w_in, b_in, w_out, ocean_mask):
    batch, rows, cols, chans = inputs.shape
    hidden = w_in.shape[1]
    shape = jax.ShapeDtypeStruct
    taps = jnp.broadcast_to(kernel_dw.astype(F32).reshape(KS * KS, 1, chans), (KS * KS, 8, chans))
    blocks = ocean_mask.reshape(-1)
    mask = jnp.broadcast_to(
        jnp.repeat(blocks, cols // blocks.shape[0])[:, None], (cols, chans)
    ).astype(BF16)
    ext_shape = pltpu.VMEM((rows + 2 * HALF, cols + 2 * OFF, chans), F32)
    northern = lax.axis_index("lat") == lax.axis_size("lat") - 1
    is_north = jnp.where(northern, 1.0, 0.0).astype(F32).reshape(1)
    work = 2 * KS * KS * rows * cols * chans * 128
    in_share = chans // lax.axis_size("dp")
    out_share = hidden // lax.axis_size("dp")
    sums, grads = None, []
    for n in range(batch):
        tile, cot = inputs[n], cotangent[n]
        edge = row_halo(tile)
        frame = (*edge, *column_halo(tile, *edge))
        dy, g_in, g_out, g_chan, g_bin = call(
            cells_kernel,
            (
                shape(tile.shape, BF16),
                shape((chans, hidden), F32),
                shape((hidden, chans), F32),
                shape((3, chans), F32),
                shape((1, hidden), F32),
            ),
            [
                ext_shape,
                pltpu.VMEM((rows, cols, chans), F32),
                pltpu.VMEM((3, 8, chans), F32),
                pltpu.VMEM((8, hidden), F32),
            ],
            work,
            tile, *frame, cot, mask, taps, bias_dw[None], gain[None], shift_ln[None],
            w_in, b_in[None], w_out,
        )
        halves = (
            dp_share(g_in, in_share).reshape(-1, chans),
            dp_share(g_out, out_share),
            axis_sum(jnp.concatenate([g_chan, g_bin.reshape(-1, chans)], 0), "dp"),
        )

        def taps_call(first, last, dy):
            return call(
                functools.partial(taps_kernel, first, last),
                shape((KS * (last - first), chans), F32),
                [ext_shape, pltpu.VMEM((rows + 2 * (KS - 1), cols, chans), F32)],
                work // 2,
                tile, *frame, dy,
            )

        taps_low = taps_call(0, 4, dy)
        dy, south, north, *halves = lax.optimization_barrier((dy, *row_halo(dy), *halves))
        strips = column_halo(dy, south, north)
        cell_sum = axis_sum(jnp.concatenate(halves, 0), "lat")
        g_taps = jnp.concatenate([taps_low, taps_call(4, KS, dy)], 0)
        grads.append(
            call(
                input_kernel,
                shape(tile.shape, BF16),
                [
                    ext_shape,
                    pltpu.VMEM((HALF, cols + 2 * OFF, chans), F32),
                    pltpu.VMEM((HALF, cols, chans), F32),
                ],
                work,
                dy, south, north, *strips, cot, taps, is_north, scalars=1,
            )
        )
        own = (cell_sum, g_taps)
        sums = own if sums is None else tuple(s + o for s, o in zip(sums, own))
    total = axis_sum(jnp.concatenate(sums, 0), "lon")
    cells_all = lax.axis_size("dp") * batch * lax.axis_size("lat") * rows * lax.axis_size("lon") * cols
    scale = 1.0 / math.sqrt(cells_all)
    in_rows = in_share * hidden // chans
    parts = jnp.split(total, (in_rows, in_rows + out_share, in_rows + out_share + 3, total.shape[0] - KS * KS))
    s_in, s_out, s_chan, s_bin, s_taps = parts
    s_in, s_bin = s_in.reshape(in_share, hidden), s_bin.reshape(1, hidden)
    s_taps = axis_sum(axis_sum(s_taps, "dp"), "lat")
    return (
        jnp.stack(grads),
        s_in * scale,
        s_out * scale,
        s_taps.reshape(KS, KS, chans) * scale,
        s_chan[2] * scale,
        s_chan[0] * scale,
        s_chan[1] * scale,
        s_bin[0] * scale,
    )


def solution(mesh):
    field = P(("groups", "dp"), "lat", "lon", None)
    placed = (field, field, P(), P(), P(), P(), P(), P(), P(), P("lat", "lon"))
    return jax.shard_map(
        local,
        mesh=mesh,
        in_specs=placed,
        out_specs=(
            field,
            P(("groups", "dp"), None),
            P(("groups", "dp"), None),
            P("groups", None, None),
            P("groups"),
            P("groups"),
            P("groups"),
            P("groups"),
        ),
        check_vma=False,
    )
```

```python
import functools
import math

import jax
import jax.numpy as jnp
from jax import lax
from jax.experimental import pallas as pl
from jax.experimental.pallas import tpu as pltpu
from jax.sharding import PartitionSpec as P

KS = 7
HALF = 3
EPS = 1e-06
GELU_K = 0.7978845608
GELU_C = 0.044715
OFF = 8
ROWS_OUT = 8
COLS_OUT = 32
CELL_ROWS = 8
F32 = jnp.float32
BF16 = jnp.bfloat16


def load_extended(ext, tile, south, north, west, east):
    rows, cols, _ = tile.shape

    def fill(r, carry):
        ext[r + HALF, OFF : OFF + cols, :] = tile[r].astype(F32)
        return carry

    lax.fori_loop(0, rows, fill, 0)
    for m in range(HALF):
        ext[m, OFF : OFF + cols, :] = south[m].astype(F32)
        ext[rows + HALF + m, OFF : OFF + cols, :] = north[m].astype(F32)

    def sides(r, carry):
        ext[r, OFF - HALF : OFF, :] = west[r].astype(F32)
        ext[r, OFF + cols : OFF + cols + HALF, :] = east[r].astype(F32)
        return carry

    lax.fori_loop(0, rows + 2 * HALF, sides, 0)


def conv_steps(ext, taps, rows, cols, flip, finish):
    chunks = cols // COLS_OUT

    def step(i, carry):
        r0 = (i // chunks) * ROWS_OUT
        c0 = pl.multiple_of((i % chunks) * COLS_OUT, COLS_OUT)
        acc = [None] * ROWS_OUT
        for rho in range(ROWS_OUT + KS - 1):
            for b in range(KS):
                v = ext[r0 + rho, pl.ds(c0 + (OFF - HALF + b), COLS_OUT), :]
                v = v.reshape(COLS_OUT // 8, 8, v.shape[-1])
                for a in range(KS):
                    out = rho - a
                    if 0 <= out < ROWS_OUT:
                        t = a * KS + b
                        k = taps[KS * KS - 1 - t if flip else t]
                        term = v * k[None]
                        acc[out] = term if acc[out] is None else acc[out] + term
            if rho >= KS - 1:
                out = rho - (KS - 1)
                finish(r0 + out, c0, acc[out].reshape(COLS_OUT, acc[out].shape[-1]))
        return carry

    lax.fori_loop(0, (rows // ROWS_OUT) * chunks, step, 0)


def partial_sum(x):
    return jnp.sum(x.reshape(x.shape[0] // 8, 8, x.shape[1]), axis=0)


def cells_kernel(
    tile, south, north, west, east, cot, mask, taps, bias, gain, shift, w_in, b_in, w_out,
    dy, g_in, g_out, g_chan, g_bin,
    ext, y, s_chan, s_bin,
):
    rows, cols, chans = tile.shape
    hidden = w_in.shape[1]
    load_extended(ext, tile, south, north, west, east)
    bias_row = bias[...]

    def finish(r, c0, acc):
        y[r, pl.ds(c0, COLS_OUT), :] = acc + bias_row

    conv_steps(ext, taps, rows, cols, False, finish)
    g_in[...] = jnp.zeros_like(g_in)
    g_out[...] = jnp.zeros_like(g_out)
    s_chan[...] = jnp.zeros_like(s_chan)
    s_bin[...] = jnp.zeros_like(s_bin)
    count = CELL_ROWS * cols
    inv = 1.0 / chans

    def step(i, carry):
        r0 = i * CELL_ROWS
        yc = y[pl.ds(r0, CELL_ROWS)].reshape(count, chans)
        center = yc - jnp.sum(yc, -1, keepdims=True) * inv
        rstd = lax.rsqrt(jnp.sum(center * center, -1, keepdims=True) * inv + EPS)
        nhat = center * rstd
        normed = (nhat * gain[...] + shift[...]).astype(BF16)
        pre = jnp.dot(normed, w_in[...], preferred_element_type=F32) + b_in[...]
        square = pre * pre
        t = jnp.tanh(pre * (GELU_K + (GELU_K * GELU_C) * square))
        h = 0.5 + 0.5 * t
        act = pre * h
        slope = h + act * (1.0 - h) * (2.0 * GELU_K + (6.0 * GELU_K * GELU_C) * square)
        og = (cot[pl.ds(r0, CELL_ROWS)] * mask[...][None]).reshape(count, chans)
        g_out[...] += lax.dot_general(
            act.astype(BF16), og, (((0,), (0,)), ((), ())), preferred_element_type=F32
        )
        dact = lax.dot_general(
            og, w_out[...], (((1,), (1,)), ((), ())), preferred_element_type=F32
        )
        dpre = dact * slope
        dpre_b = dpre.astype(BF16)
        s_bin[...] += partial_sum(dpre)
        g_in[...] += lax.dot_general(
            normed, dpre_b, (((0,), (0,)), ((), ())), preferred_element_type=F32
        )
        dnorm = lax.dot_general(
            dpre_b, w_in[...], (((1,), (1,)), ((), ())), preferred_element_type=F32
        )
        s_chan[0] += partial_sum(dnorm * nhat)
        s_chan[1] += partial_sum(dnorm)
        dn = dnorm * gain[...]
        m1 = jnp.sum(dn, -1, keepdims=True) * inv
        m2 = jnp.sum(dn * nhat, -1, keepdims=True) * inv
        delta = (rstd * (dn - m1 - nhat * m2)).astype(BF16)
        s_chan[2] += partial_sum(delta.astype(F32))
        dy[pl.ds(r0, CELL_ROWS)] = delta.reshape(CELL_ROWS, cols, chans)
        return carry

    lax.fori_loop(0, rows // CELL_ROWS, step, 0)
    for q in range(3):
        g_chan[q : q + 1, :] = jnp.sum(s_chan[q], axis=0, keepdims=True)
    g_bin[...] = jnp.sum(s_bin[...], axis=0, keepdims=True)


def taps_kernel(first, last, tile, south, north, west, east, dy, g_taps, ext, dyf):
    rows, cols, chans = tile.shape
    load_extended(ext, tile, south, north, west, east)
    edge = jnp.zeros((cols, chans), F32)
    for m in range(KS - 1):
        dyf[m] = edge
        dyf[rows + KS - 1 + m] = edge

    def fill(r, carry):
        dyf[r + KS - 1] = dy[r].astype(F32)
        return carry

    lax.fori_loop(0, rows, fill, 0)

    def row_step(rho, acc):
        def col_step(j, acc):
            acc = list(acc)
            for sub in range(8):
                c0 = pl.multiple_of(j * 64 + sub * 8, 8)
                d = [dyf[rho + (KS - 1) - a, pl.ds(c0, 8), :] for a in range(first, last)]
                for b in range(KS):
                    v = ext[rho, pl.ds(c0 + (OFF - HALF + b), 8), :]
                    for q in range(last - first):
                        at = q * KS + b
                        acc[at] = acc[at] + v * d[q]
            return tuple(acc)

        return lax.fori_loop(0, cols // 64, col_step, acc)

    zero = jnp.zeros((8, chans), F32)
    acc = lax.fori_loop(0, rows + KS - 1, row_step, (zero,) * (KS * (last - first)))
    for n, value in enumerate(acc):
        g_taps[n : n + 1, :] = jnp.sum(value, axis=0, keepdims=True)


def input_kernel(tile, south, north, west, east, cot, taps, is_north, out, ext, fold, total):
    rows, cols, chans = tile.shape
    load_extended(ext, tile, south, north, west, east)
    flag = is_north[0]
    for m in range(HALF):
        row = ext[rows + HALF + m]
        fold[m] = row * flag
        ext[rows + HALF + m] = row * (1.0 - flag)

    def finish(r, c0, acc):
        summed = acc + cot[r, pl.ds(c0, COLS_OUT), :].astype(F32)
        out[r, pl.ds(c0, COLS_OUT), :] = summed.astype(BF16)

        @pl.when(r >= rows - HALF)
        def _():
            total[r - (rows - HALF), pl.ds(c0, COLS_OUT), :] = summed

    conv_steps(ext, taps, rows, cols, True, finish)

    def fold_step(i, carry):
        c0 = pl.multiple_of(i * COLS_OUT, COLS_OUT)
        for m in range(HALF):
            acc = total[m, pl.ds(c0, COLS_OUT), :].reshape(COLS_OUT // 8, 8, chans)
            for n in range(m + 1):
                a = KS - 1 - m + n
                for b in range(KS):
                    v = fold[n, pl.ds(c0 + (OFF - HALF + b), COLS_OUT), :]
                    acc = acc + v.reshape(COLS_OUT // 8, 8, chans) * taps[a * KS + b][None]
            out[rows - HALF + m, pl.ds(c0, COLS_OUT), :] = acc.reshape(COLS_OUT, chans).astype(BF16)
        return carry

    lax.fori_loop(0, cols // COLS_OUT, fold_step, 0)


def row_halo(tile):
    rows = tile.shape[0]
    lats, lons = lax.axis_size("lat"), lax.axis_size("lon")
    low, high = tile[:HALF], tile[rows - HALF :]
    lat = lax.axis_index("lat")
    if lats % 2:
        south = lax.ppermute(high, "lat", [(i, i + 1) for i in range(lats - 1)])
        above = lax.ppermute(low, "lat", [(i + 1, i) for i in range(lats - 1)])
        mirror = lax.ppermute(high, "lon", [(i, lons - 1 - i) for i in range(lons)])
        north = jnp.where(lat == lats - 1, mirror[::-1, ::-1, :], above)
    else:
        odd = lat % 2 == 1
        first = lax.ppermute(jnp.where(odd, low, high), "lat", [(i, i ^ 1) for i in range(lats)])
        route = []
        for j in range(lons):
            mirrored = lons - 1 - j
            route.append((j * lats + lats - 1, mirrored * lats + lats - 1))
            for i in range(1, lats - 1, 2):
                route.append((j * lats + i, j * lats + i + 1))
                route.append((j * lats + i + 1, j * lats + i))
        second = lax.ppermute(jnp.where(odd, high, low), ("lon", "lat"), route)
        folded = jnp.where(lat == lats - 1, second[::-1, ::-1, :], second)
        south = jnp.where(odd, first, second)
        north = jnp.where(odd, folded, first)
    return south, north


def column_halo(tile, south, north):
    cols, lons = tile.shape[1], lax.axis_size("lon")
    left = jnp.concatenate([south[:, :HALF], tile[:, :HALF], north[:, :HALF]], 0)
    right = jnp.concatenate([south[:, cols - HALF :], tile[:, cols - HALF :], north[:, cols - HALF :]], 0)
    west = lax.ppermute(right, "lon", [(i, (i + 1) % lons) for i in range(lons)])
    east = lax.ppermute(left, "lon", [((i + 1) % lons, i) for i in range(lons)])
    return west, east


def call(kernel, out_shape, scratch, flops, *args, scalars=0):
    vmem = pl.BlockSpec(memory_space=pltpu.VMEM)
    smem = pl.BlockSpec(memory_space=pltpu.SMEM)
    return pl.pallas_call(
        kernel,
        out_shape=out_shape,
        in_specs=[vmem] * (len(args) - scalars) + [smem] * scalars,
        out_specs=jax.tree.map(lambda _: vmem, out_shape),
        scratch_shapes=scratch,
        compiler_params=pltpu.CompilerParams(vmem_limit_bytes=56 * 1024 * 1024),
        cost_estimate=pl.CostEstimate(flops=flops, bytes_accessed=12 << 20, transcendentals=0),
    )(*args)


def axis_sum(x, axis):
    count = lax.axis_size(axis)
    if count & (count - 1):
        return lax.psum(x, axis)
    step = 1
    while step < count:
        x = x + lax.ppermute(x, axis, [(i, i ^ step) for i in range(count)])
        step *= 2
    return x


def dp_share(x, share):
    count, at = lax.axis_size("dp"), lax.axis_index("dp")
    if count != 2:
        return lax.dynamic_slice_in_dim(lax.psum(x, "dp"), at * share, share, 0)
    mine = lax.dynamic_slice_in_dim(x, at * share, share, 0)
    theirs = lax.dynamic_slice_in_dim(x, (1 - at) * share, share, 0)
    return mine + lax.ppermute(theirs, "dp", [(0, 1), (1, 0)])


def local(inputs, cotangent, kernel_dw, bias_dw, gain, shift_ln, w_in, b_in, w_out, ocean_mask):
    batch, rows, cols, chans = inputs.shape
    hidden = w_in.shape[1]
    shape = jax.ShapeDtypeStruct
    taps = jnp.broadcast_to(kernel_dw.astype(F32).reshape(KS * KS, 1, chans), (KS * KS, 8, chans))
    blocks = ocean_mask.reshape(-1)
    mask = jnp.broadcast_to(
        jnp.repeat(blocks, cols // blocks.shape[0])[:, None], (cols, chans)
    ).astype(BF16)
    ext_shape = pltpu.VMEM((rows + 2 * HALF, cols + 2 * OFF, chans), F32)
    northern = lax.axis_index("lat") == lax.axis_size("lat") - 1
    is_north = jnp.where(northern, 1.0, 0.0).astype(F32).reshape(1)
    work = 2 * KS * KS * rows * cols * chans * 128
    in_share = chans // lax.axis_size("dp")
    out_share = hidden // lax.axis_size("dp")
    sums, grads = None, []
    for n in range(batch):
        tile, cot = inputs[n], cotangent[n]
        edge = row_halo(tile)
        frame = (*edge, *column_halo(tile, *edge))
        dy, g_in, g_out, g_chan, g_bin = call(
            cells_kernel,
            (
                shape(tile.shape, BF16),
                shape((chans, hidden), F32),
                shape((hidden, chans), F32),
                shape((3, chans), F32),
                shape((1, hidden), F32),
            ),
            [
                ext_shape,
                pltpu.VMEM((rows, cols, chans), F32),
                pltpu.VMEM((3, 8, chans), F32),
                pltpu.VMEM((8, hidden), F32),
            ],
            work,
            tile, *frame, cot, mask, taps, bias_dw[None], gain[None], shift_ln[None],
            w_in, b_in[None], w_out,
        )
        halves = (
            dp_share(g_in, in_share).reshape(-1, chans),
            dp_share(g_out, out_share),
            axis_sum(jnp.concatenate([g_chan, g_bin.reshape(-1, chans)], 0), "dp"),
        )

        def taps_call(first, last, dy):
            return call(
                functools.partial(taps_kernel, first, last),
                shape((KS * (last - first), chans), F32),
                [ext_shape, pltpu.VMEM((rows + 2 * (KS - 1), cols, chans), F32)],
                work // 2,
                tile, *frame, dy,
            )

        taps_low = taps_call(0, 4, dy)
        dy, south, north, *halves = lax.optimization_barrier((dy, *row_halo(dy), *halves))
        strips = column_halo(dy, south, north)
        cell_sum = axis_sum(jnp.concatenate(halves, 0), "lat")
        g_taps = jnp.concatenate([taps_low, taps_call(4, KS, dy)], 0)
        grads.append(
            call(
                input_kernel,
                shape(tile.shape, BF16),
                [
                    ext_shape,
                    pltpu.VMEM((HALF, cols + 2 * OFF, chans), F32),
                    pltpu.VMEM((HALF, cols, chans), F32),
                ],
                work,
                dy, south, north, *strips, cot, taps, is_north, scalars=1,
            )
        )
        own = (cell_sum, g_taps)
        sums = own if sums is None else tuple(s + o for s, o in zip(sums, own))
    total = axis_sum(jnp.concatenate(sums, 0), "lon")
    cells_all = lax.axis_size("dp") * batch * lax.axis_size("lat") * rows * lax.axis_size("lon") * cols
    scale = 1.0 / math.sqrt(cells_all)
    in_rows = in_share * hidden // chans
    parts = jnp.split(total, (in_rows, in_rows + out_share, in_rows + out_share + 3, total.shape[0] - KS * KS))
    s_in, s_out, s_chan, s_bin, s_taps = parts
    s_in, s_bin = s_in.reshape(in_share, hidden), s_bin.reshape(1, hidden)
    s_taps = axis_sum(axis_sum(s_taps, "dp"), "lat")
    return (
        jnp.stack(grads),
        s_in * scale,
        s_out * scale,
        s_taps.reshape(KS, KS, chans) * scale,
        s_chan[2] * scale,
        s_chan[0] * scale,
        s_chan[1] * scale,
        s_bin[0] * scale,
    )


def solution(mesh):
    field = P(("groups", "dp"), "lat", "lon", None)
    placed = (field, field, P(), P(), P(), P(), P(), P(), P(), P("lat", "lon"))
    return jax.shard_map(
        local,
        mesh=mesh,
        in_specs=placed,
        out_specs=(
            field,
            P(("groups", "dp"), None),
            P(("groups", "dp"), None),
            P("groups", None, None),
            P("groups"),
            P("groups"),
            P("groups"),
            P("groups"),
        ),
        check_vma=False,
    )
```
